512 devices in a mesh: depth: 8 (over z_hi, x), gx: 8 (over y), gy: 8 (over z_lo, core).
Axes of the slice: x: 4, y: 8, z: 8 (z_hi: 2, z_lo: 4; z = z_hi * 4 + z_lo), core: 2. Of those that a mesh axis runs over, the one named last changes fastest.
Arguments:
- arrival: bfloat16 [8, 192, 8, 8, 896], P('depth', None, 'gx', 'gy'), may hold values from -6 to 6
- source: bfloat16 [8, 4, 192, 8, 8, 896], P('depth', None, None, 'gx', 'gy'), may hold values from -6 to 6
- assignment: int32 [4, 192], replicated, may hold values from 0 to 191, each once within a row
- counts: int32 [11, 12, 8, 8], P(None, None, 'gx', 'gy'), may hold values from 1 to 16
- first_map: bfloat16 [8, 8, 8, 896, 896], P('depth', 'gx', 'gy'), may hold values from -0.1875 to 0.1875
- second_map: bfloat16 [8, 8, 8, 896, 896], P('depth', 'gx', 'gy'), may hold values from -0.1875 to 0.1875
- damping: float32 [8, 8, 8, 896], P('depth', 'gx', 'gy'), may hold values from 0.2 to 0.9
Outputs:
- final_traces: bfloat16 [8, 192, 8, 8, 896], P('depth', None, 'gx', 'gy')
The draws below stay inside these ranges and needn't reach their ends.
Inputs may be any that keep to these rules, and one draw needn't show every extreme that they name: Each row of assignment is a permutation of the 192 shots.
All inputs are finite; a program needn't handle non-finite values.
Results may differ from the reference program's by a relative error of at most 0.017.
Values may be sent and summed in bfloat16 or wider, within the bound.
A program may use at most 64 MiB of HBM per device.

```python
import math
import jax
import jax.numpy as jnp
from jax import lax

FX = 32
FY = 28
M = 896
SHOT_BATCH = 16
NBATCH = 12
ROUNDS = 4
SLOTS = 192
LAYERS = 8
BX = 8
BY = 8
UNITS = 11


def with_ends(values, own_key, smallest, largest):
    extent = values.shape
    spot = [jax.random.randint(jax.random.fold_in(own_key, axis), (), 0, extent[axis]) for axis in range(len(extent))]
    values = values.at[tuple(spot)].set(smallest)
    longest = extent.index(max(extent))
    spot[longest] = (spot[longest] + 1) % extent[longest]
    return values.at[tuple(spot)].set(largest)


def steps_of(stream_key, dims, pieces, smallest, largest):
    factor_of = 1.0
    for axis_at, shards_of in pieces:
        heights = jax.random.uniform(jax.random.fold_in(jax.random.fold_in(stream_key, 6), axis_at), (shards_of,), jnp.float32, smallest / len(pieces), largest / len(pieces))
        factor_of = factor_of * jnp.repeat(jnp.exp(heights), dims[axis_at] // shards_of).reshape((-1,) + (1,) * (len(dims) - 1 - axis_at))
    return factor_of


def noise(own_key, dims, width, reach, split=(), kind=jnp.bfloat16):
    values = jax.random.normal(own_key, dims, jnp.float32) * width
    if len(split) > 0:
        values = steps_of(own_key, dims, split, -0.22, 0.18) * values
    return jnp.clip(values, min=-reach, max=reach).astype(kind)


def setup_inputs(seed: int = 0) -> dict:
    keys = jax.random.split(jax.random.key(seed), 8)
    return {
        "arrival": noise(keys[0], (LAYERS, SLOTS, BX, BY, M), 1.0, 6.0, ((0, 8), (2, 8), (3, 8))),
        "source": noise(keys[1], (LAYERS, ROUNDS, SLOTS, BX, BY, M), 1.0, 6.0, ((0, 8), (3, 8), (4, 8))),
        "assignment": jax.vmap(lambda own: jax.random.permutation(own, SLOTS))(jax.random.split(keys[2], ROUNDS)).reshape((ROUNDS, SLOTS)).astype(jnp.int32),
        "counts": with_ends(jax.random.randint(keys[3], (UNITS, NBATCH, BX, BY), 1, SHOT_BATCH + 1), jax.random.fold_in(keys[3], 1), 1, SHOT_BATCH).astype(jnp.int32),
        "first_map": noise(keys[4], (LAYERS, BX, BY, M, M), M ** -0.5, 0.1875, ((0, 8), (1, 8), (2, 8))),
        "second_map": noise(keys[5], (LAYERS, BX, BY, M, M), M ** -0.5, 0.1875, ((0, 8), (1, 8), (2, 8))),
        "damping": jnp.clip(jnp.exp(math.log(0.9) - 1.50407736 * jax.random.uniform(keys[6], (LAYERS, BX, BY, M), jnp.float32) ** steps_of(keys[6], (LAYERS, BX, BY, M), ((0, 8), (1, 8), (2, 8)), -0.2, 0.2)), 0.2, 0.9),
    }


coupling_weight = 0.25


def lateral(mapped):
    slot_count = mapped.shape[0]
    face_grid = mapped.reshape(slot_count, BX, BY, FX, FY).transpose(0, 1, 3, 2, 4).reshape(slot_count, BX * FX, BY * FY)
    padded = jnp.pad(face_grid.astype(jnp.float32), ((0, 0), (1, 1), (1, 1)))
    around_sum = padded[:, 2:, 1:-1] + padded[:, :-2, 1:-1] + padded[:, 1:-1, 2:] + padded[:, 1:-1, :-2]
    regrid = around_sum.reshape(slot_count, BX, FX, BY, FY).transpose(0, 1, 3, 2, 4)
    return regrid.reshape(slot_count, BX, BY, FX * FY)


def reference(arrival, source, assignment, counts, first_map, second_map, damping):
    layer_count = arrival.shape[0]
    slot_count = arrival.shape[1]
    positions = jnp.arange(SHOT_BATCH, dtype=jnp.int32)
    incoming = arrival
    traces = arrival
    for round_number in range(ROUNDS):
        def one_layer(packed):
            layer_index, arriving, sources_now, map_first, map_second, damping_now = packed
            unit_index = (round_number - layer_index + layer_count - 1).astype(jnp.int32)
            live_counts = lax.dynamic_index_in_dim(counts, unit_index, 0, keepdims=False)
            active = (positions[None, :, None, None] < live_counts[:, None, :, :]).reshape(slot_count, BX, BY)
            active = active.astype(jnp.float32)[..., None]
            picked = jnp.take(sources_now, assignment[round_number], axis=0)
            start_trace = (active * (picked.astype(jnp.float32) + arriving.astype(jnp.float32))).astype(jnp.bfloat16)
            mapped = jnp.einsum("sijm,ijmn->sijn", start_trace.astype(jnp.float32), map_first.astype(jnp.float32)).astype(jnp.bfloat16)
            coupled = (mapped.astype(jnp.float32) + coupling_weight * lateral(mapped)).astype(jnp.bfloat16)
            imaged = jnp.einsum("sijm,ijmn->sijn", coupled.astype(jnp.float32), map_second.astype(jnp.float32))
            blended = damping_now * imaged + (1.0 - damping_now) * start_trace.astype(jnp.float32)
            return (active * blended).astype(jnp.bfloat16)

        traces = lax.map(one_layer, (jnp.arange(layer_count, dtype=jnp.int32), incoming, source[:, round_number], first_map, second_map, damping))
        incoming = jnp.concatenate([jnp.zeros_like(traces[:1]), traces[:-1]], axis=0)
    return traces
```

```python
import jax
import jax.numpy as jnp
from jax import lax
from jax.experimental import pallas as pl
from jax.experimental.pallas import tpu as pltpu
from jax.sharding import PartitionSpec as P

FX = 32
FY = 28
M = FX * FY
SHOT_BATCH = 16
SLOTS = 192
ROUNDS = 4

CHUNKS = 4
CH = SLOTS // CHUNKS
NB = CH // SHOT_BATCH
LANES = 128
coupling_weight = 0.25

MESH = pl.DeviceIdType.MESH
BF = jnp.bfloat16
F32 = jnp.float32

CROSS_FROM = 3
CROSS_TO = 4
CROSS_VIA = 0
RELAY = True


def cross_cut(c):
    return 512 if c % 2 == 0 else 384


def own_face_cell(k):
    return jnp.where(
        k < 32,
        jnp.where(k < FY, k, -1),
        jnp.where(
            k < 64,
            jnp.where(k < 32 + FY, M - FY + k - 32, -1),
            jnp.where(k < 96, (k - 64) * FY, (k - 96) * FY + FY - 1),
        ),
    )


def far_face_cell(k):
    return jnp.where(
        k < 32,
        jnp.where(k < FY, M - FY + k, -1),
        jnp.where(
            k < 64,
            jnp.where(k < 32 + FY, k - 32, -1),
            jnp.where(k < 96, (k - 64) * FY + FY - 1, (k - 96) * FY),
        ),
    )


def kernel(
    arrival_ref,
    source_ref,
    assign_ref,
    counts_ref,
    first_ref,
    second_ref,
    damping_ref,
    out_ref,
    inc_v,
    src_v,
    first_v,
    second_v,
    pick_v,
    face_sel_v,
    halo_sel_v,
    start_v,
    mapped_v,
    faces_v,
    halo_v,
    h_v,
    relay_v,
    load_sem,
    face_send,
    face_recv,
    down_send,
    down_recv,
    relay_send,
    relay_recv,
    relay_out,
    relay_in,
    out_sem,
):
    depth = lax.axis_index("depth")
    gx = lax.axis_index("gx")
    gy = lax.axis_index("gy")
    layers = lax.axis_size("depth")
    sides = []
    for axis, at in (("gx", gx), ("gy", gy)):
        size = lax.axis_size(axis)
        sides.append((axis, at - 1, at > 0))
        sides.append((axis, at + 1, at < size - 1))
    has_up = depth > 0
    has_down = depth < layers - 1

    barrier = pltpu.get_barrier_semaphore()
    partners = [(axis, to, there) for axis, to, there in sides]
    partners.append(("depth", depth - 1, has_up))
    partners.append(("depth", depth + 1, has_down))
    relaying = RELAY and layers > CROSS_TO
    if relaying:
        partners.append(("depth", CROSS_VIA, depth == CROSS_FROM))
        partners.append(("depth", CROSS_FROM, depth == CROSS_VIA))
        partners.append(("depth", CROSS_TO, depth == CROSS_VIA))
        partners.append(("depth", CROSS_VIA, depth == CROSS_TO))
    for axis, to, there in partners:

        @pl.when(there)
        def _():
            pl.semaphore_signal(barrier, inc=1, device_id={axis: to}, device_id_type=MESH)

    def load(src, dst, at):
        return pltpu.make_async_copy(src, dst, load_sem.at[at])

    loads = [
        load(source_ref.at[pl.ds(0, SLOTS)], src_v.at[pl.ds(0, SLOTS)], 0),
        load(arrival_ref, inc_v.at[pl.ds(0, SLOTS)], 1),
        load(first_ref, first_v, 2),
        load(second_ref, second_v, 3),
        load(source_ref.at[pl.ds(SLOTS, 3 * SLOTS)], src_v.at[pl.ds(SLOTS, 3 * SLOTS)], 4),
    ]
    for one in loads:
        one.start()

    sub = lax.broadcasted_iota(jnp.int32, (SLOTS, SLOTS), 0)
    lane = lax.broadcasted_iota(jnp.int32, (SLOTS, SLOTS), 1)
    for r in range(ROUNDS):
        row = jnp.broadcast_to(assign_ref[r : r + 1, :].astype(F32), (SLOTS, SLOTS))
        column = jnp.sum(jnp.where(sub == lane, row, 0.0), axis=1, keepdims=True)
        pick_v[r * SLOTS : (r + 1) * SLOTS, :] = (column == lane.astype(F32)).astype(F32).astype(BF)
    cells = lax.broadcasted_iota(jnp.int32, (M, LANES), 0)
    faces = own_face_cell(lax.broadcasted_iota(jnp.int32, (M, LANES), 1))
    face_sel_v[...] = (cells == faces).astype(F32).astype(BF)
    cells = lax.broadcasted_iota(jnp.int32, (LANES, M), 1)
    faces = far_face_cell(lax.broadcasted_iota(jnp.int32, (LANES, M), 0))
    halo_sel_v[...] = (cells == faces).astype(F32).astype(BF)

    for k, (_, _, there) in enumerate(sides):

        @pl.when(jnp.logical_not(there))
        def _():
            halo_v[k] = jnp.zeros((ROUNDS * SLOTS, LANES), BF)

    @pl.when(jnp.logical_not(has_up))
    def _():
        inc_v[pl.ds(SLOTS, 3 * SLOTS), :] = jnp.zeros((3 * SLOTS, M), BF)

    def rows_of(t):
        return pl.ds(pl.multiple_of(t * CH, SHOT_BATCH), CH)

    def active_of(r, c):
        unit = r - depth + layers - 1
        inside = lax.broadcasted_iota(jnp.int32, (CH, LANES), 0)
        limit = jnp.broadcast_to(counts_ref[unit, c * NB], (CH, LANES))
        for b in range(1, NB):
            limit = jnp.where(
                inside < b * SHOT_BATCH, limit, counts_ref[unit, c * NB + b] + b * SHOT_BATCH
            )
        return jnp.concatenate([inside < limit] * (M // LANES), axis=1)

    def face_copy(k, t):
        axis, to, _ = sides[k]
        return pltpu.make_async_remote_copy(
            src_ref=faces_v.at[rows_of(t)],
            dst_ref=halo_v.at[k ^ 1, rows_of(t)],
            send_sem=face_send.at[k, t],
            recv_sem=face_recv.at[k ^ 1, t],
            device_id={axis: to},
            device_id_type=MESH,
        )

    def face_arrival(k, t):
        axis, to, _ = sides[k]
        return pltpu.make_async_remote_copy(
            src_ref=faces_v.at[rows_of(t)],
            dst_ref=halo_v.at[k, rows_of(t)],
            send_sem=face_send.at[k, t],
            recv_sem=face_recv.at[k, t],
            device_id={axis: to},
            device_id_type=MESH,
        )

    def down_copy(t, lanes):
        return pltpu.make_async_remote_copy(
            src_ref=h_v.at[rows_of(t), lanes],
            dst_ref=inc_v.at[rows_of(t + CHUNKS), lanes],
            send_sem=down_send.at[t],
            recv_sem=down_recv.at[t],
            device_id={"depth": depth + 1},
            device_id_type=MESH,
        )

    def to_relay(t, lanes):
        return pltpu.make_async_remote_copy(
            src_ref=h_v.at[rows_of(t), lanes],
            dst_ref=relay_v.at[rows_of(t), lanes],
            send_sem=relay_send.at[t],
            recv_sem=relay_recv.at[t],
            device_id={"depth": CROSS_VIA},
            device_id_type=MESH,
        )

    def from_relay(t, lanes):
        return pltpu.make_async_remote_copy(
            src_ref=relay_v.at[rows_of(t), lanes],
            dst_ref=inc_v.at[rows_of(t + CHUNKS), lanes],
            send_sem=relay_out.at[t],
            recv_sem=relay_in.at[t],
            device_id={"depth": CROSS_TO},
            device_id_type=MESH,
        )

    whole = pl.ds(0, M)

    def straight(c):
        return pl.ds(0, cross_cut(c))

    def passed(c):
        return pl.ds(cross_cut(c), M - cross_cut(c))

    def map_faces(r, c):
        t = r * CHUNKS + c
        rows = rows_of(t)
        if relaying:

            @pl.when((r > 0) & has_up & (depth != CROSS_TO))
            def _():
                down_copy(t - CHUNKS, whole).wait_recv()

            @pl.when((r > 0) & (depth == CROSS_TO))
            def _():
                down_copy(t - CHUNKS, straight(c)).wait_recv()
                from_relay(t - CHUNKS, passed(c)).wait_recv()

        else:

            @pl.when((r > 0) & has_up)
            def _():
                down_copy(t - CHUNKS, whole).wait_recv()

        shots = src_v[pl.ds(pl.multiple_of(r * SLOTS, SHOT_BATCH), SLOTS), :]
        picked = jnp.dot(pick_v[rows, :], shots, preferred_element_type=F32)
        start = jnp.where(active_of(r, c), picked + inc_v[rows, :].astype(F32), 0.0).astype(BF)
        start_v[rows, :] = start
        mapped = jnp.dot(start, first_v[...], preferred_element_type=F32).astype(BF)
        mapped_v[rows, :] = mapped
        faces_v[rows, :] = jnp.dot(mapped, face_sel_v[...], preferred_element_type=F32).astype(BF)

    def send_faces(r, c):
        for k, (_, _, there) in enumerate(sides):

            @pl.when(there)
            def _():
                face_copy(k, r * CHUNKS + c).start()

    def couple(r, c):
        t = r * CHUNKS + c
        rows = rows_of(t)
        for k, (_, _, there) in enumerate(sides):

            @pl.when(there)
            def _():
                face_arrival(k, t).wait_recv()

        spot = lax.broadcasted_iota(jnp.int32, (CH, LANES), 1)
        low = jnp.where(spot < 32, halo_v[1, rows, :].astype(F32), halo_v[0, rows, :].astype(F32))
        high = jnp.where(spot < 96, halo_v[3, rows, :].astype(F32), halo_v[2, rows, :].astype(F32))
        halo = jnp.where(spot < 64, low, high).astype(BF)
        around = jnp.dot(halo, halo_sel_v[...], preferred_element_type=F32)
        mapped = mapped_v[rows, :].astype(F32)
        cell = lax.broadcasted_iota(jnp.int32, (CH, M), 1)
        across = lax.rem(cell, FY)
        around += jnp.where(cell < M - FY, pltpu.roll(mapped, M - FY, 1), 0.0)
        around += jnp.where(cell >= FY, pltpu.roll(mapped, FY, 1), 0.0)
        around += jnp.where(across < FY - 1, pltpu.roll(mapped, M - 1, 1), 0.0)
        around += jnp.where(across > 0, pltpu.roll(mapped, 1, 1), 0.0)
        coupled = (mapped + coupling_weight * around).astype(BF)
        image = jnp.dot(coupled, second_v[...], preferred_element_type=F32)
        damping = damping_ref[...]
        blended = damping * image + (1.0 - damping) * start_v[rows, :].astype(F32)
        h_v[rows, :] = jnp.where(active_of(r, c), blended, 0.0).astype(BF)

        if relaying:

            @pl.when((r < ROUNDS - 1) & has_down & (depth != CROSS_FROM))
            def _():
                down_copy(t, whole).start()

            @pl.when((r < ROUNDS - 1) & (depth == CROSS_FROM))
            def _():
                to_relay(t, passed(c)).start()
                down_copy(t, straight(c)).start()

            @pl.when((r > 0) & (depth == CROSS_VIA))
            def _():
                to_relay(t - CHUNKS, passed(c)).wait_recv()
                from_relay(t - CHUNKS, passed(c)).start()

        else:

            @pl.when((r < ROUNDS - 1) & has_down)
            def _():
                down_copy(t, whole).start()

        @pl.when(r == ROUNDS - 1)
        def _():
            out_copy(t, c).start()

    def out_copy(t, c):
        return pltpu.make_async_copy(
            h_v.at[rows_of(t)], out_ref.at[pl.ds(c * CH, CH)], out_sem.at[c]
        )

    for one in loads[:3]:
        one.wait()

    def one_round(r, first):
        for c in range(CHUNKS):
            map_faces(r, c)
            if first and c == 0:
                pl.semaphore_wait(barrier, sum(there.astype(jnp.int32) for _, _, there in partners))

            send_faces(r, c)
            if c >= 2:
                if first and c == 2:
                    loads[3].wait()
                couple(r, c - 2)
        couple(r, CHUNKS - 2)
        couple(r, CHUNKS - 1)

    one_round(jnp.int32(0), True)
    loads[4].wait()

    def later_round(r, carry):
        one_round(r, False)
        return carry

    lax.fori_loop(1, ROUNDS, later_round, 0)

    for c in range(CHUNKS):
        out_copy((ROUNDS - 1) * CHUNKS + c, c).wait()

    def drain_faces(t, carry):
        for k, (_, _, there) in enumerate(sides):

            @pl.when(there)
            def _():
                face_copy(k, t).wait_send()

        return carry

    lax.fori_loop(0, ROUNDS * CHUNKS, drain_faces, 0)

    def drain_down(r, carry):
        for c in range(CHUNKS):
            t = r * CHUNKS + c
            if relaying:

                @pl.when(has_down & (depth != CROSS_FROM))
                def _():
                    down_copy(t, whole).wait_send()

                @pl.when(depth == CROSS_FROM)
                def _():
                    down_copy(t, straight(c)).wait_send()
                    to_relay(t, passed(c)).wait_send()

                @pl.when(depth == CROSS_VIA)
                def _():
                    from_relay(t, passed(c)).wait_send()

            else:

                @pl.when(has_down)
                def _():
                    down_copy(t, whole).wait_send()

        return carry

    lax.fori_loop(0, ROUNDS - 1, drain_down, 0)


def local(arrival, source, assignment, counts, first_map, second_map, damping):
    steps = ROUNDS * CHUNKS
    slots = ROUNDS * SLOTS
    anywhere = pl.BlockSpec(memory_space=pl.ANY)
    vmem = pl.BlockSpec(memory_space=pltpu.VMEM)
    dma = pltpu.SemaphoreType.DMA
    units, batches = counts.shape[:2]
    result = pl.pallas_call(
        kernel,
        out_shape=jax.ShapeDtypeStruct((SLOTS, M), BF),
        in_specs=[
            anywhere,
            anywhere,
            vmem,
            pl.BlockSpec(memory_space=pltpu.SMEM),
            anywhere,
            anywhere,
            vmem,
        ],
        out_specs=anywhere,
        scratch_shapes=[
            pltpu.VMEM((slots, M), BF),
            pltpu.VMEM((slots, M), BF),
            pltpu.VMEM((M, M), BF),
            pltpu.VMEM((M, M), BF),
            pltpu.VMEM((slots, SLOTS), BF),
            pltpu.VMEM((M, LANES), BF),
            pltpu.VMEM((LANES, M), BF),
            pltpu.VMEM((slots, M), BF),
            pltpu.VMEM((slots, M), BF),
            pltpu.VMEM((slots, LANES), BF),
            pltpu.VMEM((4, slots, LANES), BF),
            pltpu.VMEM((slots, M), BF),
            pltpu.VMEM((slots, M), BF),
            dma((5,)),
            dma((4, steps)),
            dma((4, steps)),
            dma((steps,)),
            dma((steps,)),
            dma((steps,)),
            dma((steps,)),
            dma((steps,)),
            dma((steps,)),
            dma((CHUNKS,)),
        ],
        compiler_params=pltpu.CompilerParams(collective_id=0, has_side_effects=True),
        name="sweep",
    )(
        arrival.reshape(SLOTS, M),
        source.reshape(slots, M),
        assignment,
        counts.reshape(units, batches),
        first_map.reshape(M, M),
        second_map.reshape(M, M),
        damping.reshape(1, M),
    )
    return result.reshape(1, SLOTS, 1, 1, M)


def solution(mesh):
    return jax.shard_map(
        local,
        mesh=mesh,
        in_specs=(
            P("depth", None, "gx", "gy", None),
            P("depth", None, None, "gx", "gy", None),
            P(),
            P(None, None, "gx", "gy"),
            P("depth", "gx", "gy", None, None),
            P("depth", "gx", "gy", None, None),
            P("depth", "gx", "gy", None),
        ),
        out_specs=P("depth", None, "gx", "gy", None),
        check_vma=False,
    )
```

```python
import jax
import jax.numpy as jnp
from jax import lax
from jax.experimental import pallas as pl
from jax.experimental.pallas import tpu as pltpu
from jax.sharding import PartitionSpec as P

FX = 32
FY = 28
M = FX * FY
SHOT_BATCH = 16
SLOTS = 192
ROUNDS = 4

CHUNKS = 3
CH = SLOTS // CHUNKS
NB = CH // SHOT_BATCH
LANES = 128
coupling_weight = 0.25

MESH = pl.DeviceIdType.MESH
BF = jnp.bfloat16
F32 = jnp.float32

CROSS_FROM = 3
CROSS_TO = 4
CROSS_VIA = (0, 2, 1)
SHARE = CH // (1 + len(CROSS_VIA))
RELAY = True


def own_face_cell(k):
    return jnp.where(
        k < 32,
        jnp.where(k < FY, k, -1),
        jnp.where(
            k < 64,
            jnp.where(k < 32 + FY, M - FY + k - 32, -1),
            jnp.where(k < 96, (k - 64) * FY, (k - 96) * FY + FY - 1),
        ),
    )


def far_face_cell(k):
    return jnp.where(
        k < 32,
        jnp.where(k < FY, M - FY + k, -1),
        jnp.where(
            k < 64,
            jnp.where(k < 32 + FY, k - 32, -1),
            jnp.where(k < 96, (k - 64) * FY + FY - 1, (k - 96) * FY),
        ),
    )


def kernel(
    arrival_ref,
    source_ref,
    assign_ref,
    counts_ref,
    first_ref,
    second_ref,
    damping_ref,
    out_ref,
    inc_v,
    src_v,
    first_v,
    second_v,
    pick_v,
    face_sel_v,
    halo_sel_v,
    first_faces_v,
    halo_map_v,
    weight_v,
    damping_v,
    base_v,
    faces_v,
    halo_v,
    h_v,
    relay_v,
    load_sem,
    face_send,
    face_recv,
    down_send,
    down_recv,
    relay_send,
    relay_recv,
    relay_out,
    relay_in,
    out_sem,
):
    depth = lax.axis_index("depth")
    gx = lax.axis_index("gx")
    gy = lax.axis_index("gy")
    layers = lax.axis_size("depth")
    sides = []
    for axis, at in (("gx", gx), ("gy", gy)):
        size = lax.axis_size(axis)
        sides.append((axis, at - 1, at > 0))
        sides.append((axis, at + 1, at < size - 1))
    has_up = depth > 0
    has_down = depth < layers - 1

    barrier = pltpu.get_barrier_semaphore()
    partners = [(axis, to, there) for axis, to, there in sides]
    partners.append(("depth", depth - 1, has_up))
    partners.append(("depth", depth + 1, has_down))
    relaying = RELAY and layers > CROSS_TO
    if relaying:
        for via in CROSS_VIA:
            for end in (CROSS_FROM, CROSS_TO):
                if abs(via - end) > 1:
                    partners.append(("depth", via, depth == end))
                    partners.append(("depth", end, depth == via))
    for axis, to, there in partners:

        @pl.when(there)
        def _():
            pl.semaphore_signal(barrier, inc=1, device_id={axis: to}, device_id_type=MESH)

    def load(src, dst, at):
        return pltpu.make_async_copy(src, dst, load_sem.at[at])

    loads = [
        load(source_ref.at[pl.ds(0, SLOTS)], src_v.at[pl.ds(0, SLOTS)], 0),
        load(arrival_ref, inc_v.at[pl.ds(0, SLOTS)], 1),
        load(first_ref, first_v, 2),
        load(second_ref, second_v, 3),
        load(source_ref.at[pl.ds(SLOTS, 3 * SLOTS)], src_v.at[pl.ds(SLOTS, 3 * SLOTS)], 4),
    ]
    for one in loads:
        one.start()

    sub = lax.broadcasted_iota(jnp.int32, (SLOTS, SLOTS), 0)
    lane = lax.broadcasted_iota(jnp.int32, (SLOTS, SLOTS), 1)

    def fill_pick(r):
        row = jnp.broadcast_to(assign_ref[r : r + 1, :].astype(F32), (SLOTS, SLOTS))
        column = jnp.sum(jnp.where(sub == lane, row, 0.0), axis=1, keepdims=True)
        hot = (column == lane.astype(F32)).astype(F32)
        pick_v[r * SLOTS : (r + 1) * SLOTS, :] = hot.astype(BF)

    fill_pick(0)
    cells = lax.broadcasted_iota(jnp.int32, (M, LANES), 0)
    faces = own_face_cell(lax.broadcasted_iota(jnp.int32, (M, LANES), 1))
    face_sel_v[...] = (cells == faces).astype(F32).astype(BF)
    cells = lax.broadcasted_iota(jnp.int32, (LANES, M), 1)
    faces = far_face_cell(lax.broadcasted_iota(jnp.int32, (LANES, M), 0))
    halo_sel_v[...] = (cells == faces).astype(F32).astype(BF)

    cells = lax.broadcasted_iota(jnp.int32, (8, M), 1)
    across = lax.rem(cells, FY)
    for k, inside in enumerate((cells < M - FY, cells >= FY, across < FY - 1, across > 0)):
        weight_v[k] = jnp.where(inside, coupling_weight, 0.0)
    damping_v[0] = jnp.broadcast_to(damping_ref[...], (8, M))
    damping_v[1] = 1.0 - damping_v[0]

    def on_rows(eight):
        return jnp.concatenate([eight] * (CH // 8), axis=0)

    for k, (_, _, there) in enumerate(sides):

        @pl.when(jnp.logical_not(there))
        def _():
            halo_v[k] = jnp.zeros((ROUNDS * SLOTS, LANES), BF)

    @pl.when(jnp.logical_not(has_up))
    def _():
        inc_v[pl.ds(SLOTS, 3 * SLOTS), :] = jnp.zeros((3 * SLOTS, M), BF)

    def rows_of(t):
        return pl.ds(pl.multiple_of(t * CH, SHOT_BATCH), CH)

    def active_of(r, c):
        unit = r - depth + layers - 1
        inside = lax.broadcasted_iota(jnp.int32, (CH, LANES), 0)
        limit = jnp.broadcast_to(counts_ref[unit, 0, c * NB], (CH, LANES))
        for b in range(1, NB):
            limit = jnp.where(
                inside < b * SHOT_BATCH, limit, counts_ref[unit, 0, c * NB + b] + b * SHOT_BATCH
            )
        return jnp.concatenate([inside < limit] * (M // LANES), axis=1)

    def face_copy(k, t):
        axis, to, _ = sides[k]
        return pltpu.make_async_remote_copy(
            src_ref=faces_v.at[rows_of(t)],
            dst_ref=halo_v.at[k ^ 1, rows_of(t)],
            send_sem=face_send.at[k, t],
            recv_sem=face_recv.at[k ^ 1, t],
            device_id={axis: to},
            device_id_type=MESH,
        )

    def face_arrival(k, t):
        axis, to, _ = sides[k]
        return pltpu.make_async_remote_copy(
            src_ref=faces_v.at[rows_of(t)],
            dst_ref=halo_v.at[k, rows_of(t)],
            send_sem=face_send.at[k, t],
            recv_sem=face_recv.at[k, t],
            device_id={axis: to},
            device_id_type=MESH,
        )

    def share_of(t, part):
        return pl.ds(pl.multiple_of(t * CH + part * SHARE, SHOT_BATCH), SHARE)

    def down_copy(t, share=None):
        here = rows_of(t) if share is None else share_of(t, share)
        there = rows_of(t + CHUNKS) if share is None else share_of(t + CHUNKS, share)
        return pltpu.make_async_remote_copy(
            src_ref=h_v.at[here],
            dst_ref=inc_v.at[there],
            send_sem=down_send.at[t],
            recv_sem=down_recv.at[t],
            device_id={"depth": depth + 1},
            device_id_type=MESH,
        )

    def relay_rows(t):
        return pl.ds(pl.multiple_of(t * SHARE, SHOT_BATCH), SHARE)

    def to_relay(t, q):
        return pltpu.make_async_remote_copy(
            src_ref=h_v.at[share_of(t, 1 + q)],
            dst_ref=relay_v.at[relay_rows(t)],
            send_sem=relay_send.at[q, t],
            recv_sem=relay_recv.at[t],
            device_id={"depth": CROSS_VIA[q]},
            device_id_type=MESH,
        )

    def from_relay(t, q):
        return pltpu.make_async_remote_copy(
            src_ref=relay_v.at[relay_rows(t)],
            dst_ref=inc_v.at[share_of(t + CHUNKS, 1 + q)],
            send_sem=relay_out.at[t],
            recv_sem=relay_in.at[q, t],
            device_id={"depth": CROSS_TO},
            device_id_type=MESH,
        )

    def pass_on(r, c):
        if relaying:
            t = r * CHUNKS + c
            for q, via in enumerate(CROSS_VIA):

                @pl.when((r < ROUNDS - 1) & (depth == via))
                def _():
                    to_relay(t, q).wait_recv()
                    from_relay(t, q).start()

    def advance(r, c, first):
        t = r * CHUNKS + c
        rows = rows_of(t)
        shots = src_v[pl.ds(pl.multiple_of(r * SLOTS, SHOT_BATCH), SLOTS), :]
        picked = jnp.dot(pick_v[rows, :], shots, preferred_element_type=F32)
        if relaying:

            @pl.when((r > 0) & has_up & (depth != CROSS_TO))
            def _():
                down_copy(t - CHUNKS).wait_recv()

            @pl.when((r > 0) & (depth == CROSS_TO))
            def _():
                down_copy(t - CHUNKS, 0).wait_recv()
                for q in range(len(CROSS_VIA)):
                    from_relay(t - CHUNKS, q).wait_recv()

        else:

            @pl.when((r > 0) & has_up)
            def _():
                down_copy(t - CHUNKS).wait_recv()

        start = jnp.where(active_of(r, c), picked + inc_v[rows, :].astype(F32), 0.0).astype(BF)
        if first:
            mapped = jnp.dot(start, first_v[...], preferred_element_type=F32).astype(BF)
            faces_v[rows, :] = jnp.dot(mapped, face_sel_v[...], preferred_element_type=F32).astype(BF)
            if c == 0:
                peers = sum(there.astype(jnp.int32) for _, _, there in partners)
                pl.semaphore_wait(barrier, peers)
            send_faces(r, c)
            if c == 0:
                loads[3].wait()
        else:
            faces = jnp.dot(start, first_faces_v[...], preferred_element_type=F32)
            faces_v[rows, :] = faces.astype(BF)
            send_faces(r, c)
            mapped = jnp.dot(start, first_v[...], preferred_element_type=F32).astype(BF)
        mapped = mapped.astype(F32)
        coupled = mapped
        for k, by in enumerate((M - FY, FY, M - 1, 1)):
            coupled += on_rows(weight_v[k]) * pltpu.roll(mapped, by, 1)
        image = jnp.dot(coupled.astype(BF), second_v[...], preferred_element_type=F32)
        base = on_rows(damping_v[0]) * image + on_rows(damping_v[1]) * start.astype(F32)
        base_v[c * CH : (c + 1) * CH, :] = base

    def send_faces(r, c):
        for k, (_, _, there) in enumerate(sides):

            @pl.when(there)
            def _():
                face_copy(k, r * CHUNKS + c).start()

    def finish(r, c):
        t = r * CHUNKS + c
        rows = rows_of(t)
        for k, (_, _, there) in enumerate(sides):

            @pl.when(there)
            def _():
                face_arrival(k, t).wait_recv()

        spot = lax.broadcasted_iota(jnp.int32, (CH, LANES), 1)
        low = jnp.where(spot < 32, halo_v[1, rows, :].astype(F32), halo_v[0, rows, :].astype(F32))
        high = jnp.where(spot < 96, halo_v[3, rows, :].astype(F32), halo_v[2, rows, :].astype(F32))
        halo = jnp.where(spot < 64, low, high).astype(BF)
        added = jnp.dot(halo, halo_map_v[...], preferred_element_type=F32)
        blended = base_v[c * CH : (c + 1) * CH, :] + on_rows(damping_v[0]) * added
        h_v[rows, :] = jnp.where(active_of(r, c), blended, 0.0).astype(BF)

        if relaying:

            @pl.when((r < ROUNDS - 1) & has_down & (depth != CROSS_FROM))
            def _():
                down_copy(t).start()

            @pl.when((r < ROUNDS - 1) & (depth == CROSS_FROM))
            def _():
                for q in range(len(CROSS_VIA)):
                    to_relay(t, q).start()
                down_copy(t, 0).start()

        else:

            @pl.when((r < ROUNDS - 1) & has_down)
            def _():
                down_copy(t).start()

        @pl.when(r == ROUNDS - 1)
        def _():
            out_copy(t, c).start()

    def out_copy(t, c):
        return pltpu.make_async_copy(
            h_v.at[rows_of(t)], out_ref.at[pl.ds(c * CH, CH)], out_sem.at[c]
        )

    for one in loads[:3]:
        one.wait()

    def one_round(r, first):
        lag = 2 if first else 1
        for c in range(CHUNKS):
            advance(r, c, first)
            if c < CHUNKS - 1 and not first:
                pass_on(r - 1, c + 1)
            if c == lag and first:
                rows = jnp.dot(halo_sel_v[...], second_v[...], preferred_element_type=F32)
                halo_map_v[...] = (coupling_weight * rows).astype(BF)
            if c >= lag:
                finish(r, c - lag)
        for c in range(CHUNKS - lag, CHUNKS):
            if c == CHUNKS - 1:
                pass_on(r, 0)
            finish(r, c)

    one_round(jnp.int32(0), True)
    for r in range(1, ROUNDS):
        fill_pick(r)
    columns = jnp.dot(first_v[...], face_sel_v[...], preferred_element_type=F32)
    first_faces_v[...] = columns.astype(BF)
    loads[4].wait()

    def later_round(r, carry):
        one_round(r, False)
        return carry

    lax.fori_loop(1, ROUNDS, later_round, 0)

    for c in range(CHUNKS):
        out_copy((ROUNDS - 1) * CHUNKS + c, c).wait()

    def drain_faces(t, carry):
        for k, (_, _, there) in enumerate(sides):

            @pl.when(there)
            def _():
                face_copy(k, t).wait_send()

        return carry

    lax.fori_loop(0, ROUNDS * CHUNKS, drain_faces, 0)

    def drain_down(r, carry):
        for c in range(CHUNKS):
            t = r * CHUNKS + c
            if relaying:

                @pl.when(has_down & (depth != CROSS_FROM))
                def _():
                    down_copy(t).wait_send()

                @pl.when(depth == CROSS_FROM)
                def _():
                    down_copy(t, 0).wait_send()
                    for q in range(len(CROSS_VIA)):
                        to_relay(t, q).wait_send()

                for q, via in enumerate(CROSS_VIA):

                    @pl.when(depth == via)
                    def _():
                        from_relay(t, q).wait_send()

            else:

                @pl.when(has_down)
                def _():
                    down_copy(t).wait_send()

        return carry

    lax.fori_loop(0, ROUNDS - 1, drain_down, 0)


def local(arrival, source, assignment, counts, first_map, second_map, damping):
    steps = ROUNDS * CHUNKS
    slots = ROUNDS * SLOTS
    anywhere = pl.BlockSpec(memory_space=pl.ANY)
    vmem = pl.BlockSpec(memory_space=pltpu.VMEM)
    dma = pltpu.SemaphoreType.DMA
    units, batches = counts.shape[:2]
    result = pl.pallas_call(
        kernel,
        out_shape=pltpu.VMEM((SLOTS, M), BF),
        in_specs=[
            anywhere,
            anywhere,
            vmem,
            pl.BlockSpec(memory_space=pltpu.SMEM),
            anywhere,
            anywhere,
            vmem,
        ],
        out_specs=anywhere,
        scratch_shapes=[
            pltpu.VMEM((slots, M), BF),
            pltpu.VMEM((slots, M), BF),
            pltpu.VMEM((M, M), BF),
            pltpu.VMEM((M, M), BF),
            pltpu.VMEM((slots, SLOTS), BF),
            pltpu.VMEM((M, LANES), BF),
            pltpu.VMEM((LANES, M), BF),
            pltpu.VMEM((M, LANES), BF),
            pltpu.VMEM((LANES, M), BF),
            pltpu.VMEM((4, 8, M), F32),
            pltpu.VMEM((2, 8, M), F32),
            pltpu.VMEM((SLOTS, M), F32),
            pltpu.VMEM((slots, LANES), BF),
            pltpu.VMEM((4, slots, LANES), BF),
            pltpu.VMEM((slots, M), BF),
            pltpu.VMEM((steps * SHARE, M), BF),
            dma((5,)),
            dma((4, steps)),
            dma((4, steps)),
            dma((steps,)),
            dma((steps,)),
            dma((len(CROSS_VIA), steps)),
            dma((steps,)),
            dma((steps,)),
            dma((len(CROSS_VIA), steps)),
            dma((CHUNKS,)),
        ],
        compiler_params=pltpu.CompilerParams(
            collective_id=0, has_side_effects=True, vmem_limit_bytes=60_000_000
        ),
        name="sweep",
    )(
        arrival.reshape(SLOTS, M),
        source.reshape(slots, M),
        assignment,
        counts.reshape(units, 1, batches),
        first_map.reshape(M, M),
        second_map.reshape(M, M),
        damping.reshape(1, M),
    )
    return result.reshape(1, SLOTS, 1, 1, M)


def solution(mesh):
    return jax.shard_map(
        local,
        mesh=mesh,
        in_specs=(
            P("depth", None, "gx", "gy", None),
            P("depth", None, None, "gx", "gy", None),
            P(),
            P(None, None, "gx", "gy"),
            P("depth", "gx", "gy", None, None),
            P("depth", "gx", "gy", None, None),
            P("depth", "gx", "gy", None),
        ),
        out_specs=P("depth", None, "gx", "gy", None),
        check_vma=False,
    )
```

```python
import jax
import jax.numpy as jnp
from jax import lax
from jax.experimental import pallas as pl
from jax.experimental.pallas import tpu as pltpu
from jax.sharding import PartitionSpec as P

FX = 32
FY = 28
M = FX * FY
SHOT_BATCH = 16
SLOTS = 192
ROUNDS = 4

CHUNKS = 3
CH = SLOTS // CHUNKS
NB = CH // SHOT_BATCH
LANES = 128
coupling_weight = 0.25

MESH = pl.DeviceIdType.MESH
BF = jnp.bfloat16
F32 = jnp.float32

CROSS_FROM = 3
CROSS_TO = 4
CROSS_VIA = (0, 1)
SHARE = 16
DIRECT = CH - SHARE * len(CROSS_VIA)
RELAY = True


def own_face_cell(k):
    return jnp.where(
        k < 32,
        jnp.where(k < FY, k, -1),
        jnp.where(
            k < 64,
            jnp.where(k < 32 + FY, M - FY + k - 32, -1),
            jnp.where(k < 96, (k - 64) * FY, (k - 96) * FY + FY - 1),
        ),
    )


def far_face_cell(k):
    return jnp.where(
        k < 32,
        jnp.where(k < FY, M - FY + k, -1),
        jnp.where(
            k < 64,
            jnp.where(k < 32 + FY, k - 32, -1),
            jnp.where(k < 96, (k - 64) * FY + FY - 1, (k - 96) * FY),
        ),
    )


def kernel(
    arrival_ref,
    source_ref,
    assign_ref,
    counts_ref,
    first_ref,
    second_ref,
    damping_ref,
    out_ref,
    inc_v,
    src_v,
    first_v,
    second_v,
    pick_v,
    face_sel_v,
    halo_sel_v,
    first_faces_v,
    halo_map_v,
    weight_v,
    damping_v,
    base_v,
    faces_v,
    halo_v,
    h_v,
    relay_v,
    load_sem,
    face_send,
    face_recv,
    down_send,
    down_recv,
    relay_send,
    relay_recv,
    relay_out,
    relay_in,
    out_sem,
):
    depth = lax.axis_index("depth")
    gx = lax.axis_index("gx")
    gy = lax.axis_index("gy")
    layers = lax.axis_size("depth")
    sides = []
    for axis, at in (("gx", gx), ("gy", gy)):
        size = lax.axis_size(axis)
        sides.append((axis, at - 1, at > 0))
        sides.append((axis, at + 1, at < size - 1))
    has_up = depth > 0
    has_down = depth < layers - 1

    barrier = pltpu.get_barrier_semaphore()
    partners = [(axis, to, there) for axis, to, there in sides]
    partners.append(("depth", depth - 1, has_up))
    partners.append(("depth", depth + 1, has_down))
    relaying = RELAY and layers > CROSS_TO
    if relaying:
        for via in CROSS_VIA:
            for end in (CROSS_FROM, CROSS_TO):
                if abs(via - end) > 1:
                    partners.append(("depth", via, depth == end))
                    partners.append(("depth", end, depth == via))
    for axis, to, there in partners:

        @pl.when(there)
        def _():
            pl.semaphore_signal(barrier, inc=1, device_id={axis: to}, device_id_type=MESH)

    def load(src, dst, at):
        return pltpu.make_async_copy(src, dst, load_sem.at[at])

    loads = [
        load(source_ref.at[pl.ds(0, SLOTS)], src_v.at[pl.ds(0, SLOTS)], 0),
        load(arrival_ref, inc_v.at[pl.ds(0, SLOTS)], 1),
        load(first_ref, first_v, 2),
        load(second_ref, second_v, 3),
        load(source_ref.at[pl.ds(SLOTS, 3 * SLOTS)], src_v.at[pl.ds(SLOTS, 3 * SLOTS)], 4),
    ]
    for one in loads:
        one.start()

    sub = lax.broadcasted_iota(jnp.int32, (SLOTS, SLOTS), 0)
    lane = lax.broadcasted_iota(jnp.int32, (SLOTS, SLOTS), 1)

    def fill_pick(r):
        row = jnp.broadcast_to(assign_ref[r : r + 1, :].astype(F32), (SLOTS, SLOTS))
        column = jnp.sum(jnp.where(sub == lane, row, 0.0), axis=1, keepdims=True)
        hot = (column == lane.astype(F32)).astype(F32)
        pick_v[r * SLOTS : (r + 1) * SLOTS, :] = hot.astype(BF)

    fill_pick(0)
    cells = lax.broadcasted_iota(jnp.int32, (M, LANES), 0)
    faces = own_face_cell(lax.broadcasted_iota(jnp.int32, (M, LANES), 1))
    face_sel_v[...] = (cells == faces).astype(F32).astype(BF)
    cells = lax.broadcasted_iota(jnp.int32, (LANES, M), 1)
    faces = far_face_cell(lax.broadcasted_iota(jnp.int32, (LANES, M), 0))
    halo_sel_v[...] = (cells == faces).astype(F32).astype(BF)

    cells = lax.broadcasted_iota(jnp.int32, (8, M), 1)
    across = lax.rem(cells, FY)
    for k, inside in enumerate((cells < M - FY, cells >= FY, across < FY - 1, across > 0)):
        weight_v[k] = jnp.where(inside, coupling_weight, 0.0)
    damping_v[0] = jnp.broadcast_to(damping_ref[...], (8, M))
    damping_v[1] = 1.0 - damping_v[0]

    def on_rows(eight):
        return jnp.concatenate([eight] * (CH // 8), axis=0)

    for k, (_, _, there) in enumerate(sides):

        @pl.when(jnp.logical_not(there))
        def _():
            halo_v[k] = jnp.zeros((ROUNDS * SLOTS, LANES), BF)

    @pl.when(jnp.logical_not(has_up))
    def _():
        inc_v[pl.ds(SLOTS, 3 * SLOTS), :] = jnp.zeros((3 * SLOTS, M), BF)

    def rows_of(t):
        return pl.ds(pl.multiple_of(t * CH, SHOT_BATCH), CH)

    def active_of(r, c):
        unit = r - depth + layers - 1
        inside = lax.broadcasted_iota(jnp.int32, (CH, LANES), 0)
        limit = jnp.broadcast_to(counts_ref[unit, 0, c * NB], (CH, LANES))
        for b in range(1, NB):
            limit = jnp.where(
                inside < b * SHOT_BATCH, limit, counts_ref[unit, 0, c * NB + b] + b * SHOT_BATCH
            )
        return jnp.concatenate([inside < limit] * (M // LANES), axis=1)

    def face_copy(k, t):
        axis, to, _ = sides[k]
        return pltpu.make_async_remote_copy(
            src_ref=faces_v.at[rows_of(t)],
            dst_ref=halo_v.at[k ^ 1, rows_of(t)],
            send_sem=face_send.at[k, t],
            recv_sem=face_recv.at[k ^ 1, t],
            device_id={axis: to},
            device_id_type=MESH,
        )

    def face_arrival(k, t):
        axis, to, _ = sides[k]
        return pltpu.make_async_remote_copy(
            src_ref=faces_v.at[rows_of(t)],
            dst_ref=halo_v.at[k, rows_of(t)],
            send_sem=face_send.at[k, t],
            recv_sem=face_recv.at[k, t],
            device_id={axis: to},
            device_id_type=MESH,
        )

    def share_of(t, part):
        if part == 0:
            return pl.ds(pl.multiple_of(t * CH, SHOT_BATCH), DIRECT)
        first_row = t * CH + DIRECT + (part - 1) * SHARE
        return pl.ds(pl.multiple_of(first_row, SHOT_BATCH), SHARE)

    def down_copy(t, share=None):
        here = rows_of(t) if share is None else share_of(t, share)
        there = rows_of(t + CHUNKS) if share is None else share_of(t + CHUNKS, share)
        return pltpu.make_async_remote_copy(
            src_ref=h_v.at[here],
            dst_ref=inc_v.at[there],
            send_sem=down_send.at[t],
            recv_sem=down_recv.at[t],
            device_id={"depth": depth + 1},
            device_id_type=MESH,
        )

    def relay_rows(t):
        return pl.ds(pl.multiple_of(t * SHARE, SHOT_BATCH), SHARE)

    def to_relay(t, q):
        return pltpu.make_async_remote_copy(
            src_ref=h_v.at[share_of(t, 1 + q)],
            dst_ref=relay_v.at[relay_rows(t)],
            send_sem=relay_send.at[q, t],
            recv_sem=relay_recv.at[t],
            device_id={"depth": CROSS_VIA[q]},
            device_id_type=MESH,
        )

    def from_relay(t, q):
        return pltpu.make_async_remote_copy(
            src_ref=relay_v.at[relay_rows(t)],
            dst_ref=inc_v.at[share_of(t + CHUNKS, 1 + q)],
            send_sem=relay_out.at[t],
            recv_sem=relay_in.at[q, t],
            device_id={"depth": CROSS_TO},
            device_id_type=MESH,
        )

    def pass_on(r, c):
        if relaying:
            t = r * CHUNKS + c
            for q, via in enumerate(CROSS_VIA):

                @pl.when((r < ROUNDS - 1) & (depth == via))
                def _():
                    to_relay(t, q).wait_recv()
                    from_relay(t, q).start()

    def advance(r, c, first):
        t = r * CHUNKS + c
        rows = rows_of(t)
        shots = src_v[pl.ds(pl.multiple_of(r * SLOTS, SHOT_BATCH), SLOTS), :]
        picked = jnp.dot(pick_v[rows, :], shots, preferred_element_type=F32)
        if relaying:

            @pl.when((r > 0) & has_up & (depth != CROSS_TO))
            def _():
                down_copy(t - CHUNKS).wait_recv()

            @pl.when((r > 0) & (depth == CROSS_TO))
            def _():
                down_copy(t - CHUNKS, 0).wait_recv()
                for q in range(len(CROSS_VIA)):
                    from_relay(t - CHUNKS, q).wait_recv()

        else:

            @pl.when((r > 0) & has_up)
            def _():
                down_copy(t - CHUNKS).wait_recv()

        start = jnp.where(active_of(r, c), picked + inc_v[rows, :].astype(F32), 0.0).astype(BF)
        if first:
            mapped = jnp.dot(start, first_v[...], preferred_element_type=F32).astype(BF)
            faces_v[rows, :] = jnp.dot(mapped, face_sel_v[...], preferred_element_type=F32).astype(BF)
            if c == 0:
                peers = sum(there.astype(jnp.int32) for _, _, there in partners)
                pl.semaphore_wait(barrier, peers)
            send_faces(r, c)
            if c == 0:
                loads[3].wait()
        else:
            faces = jnp.dot(start, first_faces_v[...], preferred_element_type=F32)
            faces_v[rows, :] = faces.astype(BF)
            send_faces(r, c)
            if relaying and c == 0:

                @pl.when(depth == CROSS_FROM)
                def _():
                    down_copy(t - 1, 0).start()

            if relaying and c == 2:

                @pl.when((r < ROUNDS - 1) & (depth == CROSS_FROM))
                def _():
                    down_copy(t - 2, 0).start()

            mapped = jnp.dot(start, first_v[...], preferred_element_type=F32).astype(BF)
        mapped = mapped.astype(F32)
        coupled = mapped
        for k, by in enumerate((M - FY, FY, M - 1, 1)):
            coupled += on_rows(weight_v[k]) * pltpu.roll(mapped, by, 1)
        image = jnp.dot(coupled.astype(BF), second_v[...], preferred_element_type=F32)
        base = on_rows(damping_v[0]) * image + on_rows(damping_v[1]) * start.astype(F32)
        base_v[c * CH : (c + 1) * CH, :] = base

    def send_faces(r, c):
        for k, (_, _, there) in enumerate(sides):

            @pl.when(there)
            def _():
                face_copy(k, r * CHUNKS + c).start()

    def finish(r, c, first):
        t = r * CHUNKS + c
        rows = rows_of(t)
        for k, (_, _, there) in enumerate(sides):

            @pl.when(there)
            def _():
                face_arrival(k, t).wait_recv()

        spot = lax.broadcasted_iota(jnp.int32, (CH, LANES), 1)
        low = jnp.where(spot < 32, halo_v[1, rows, :].astype(F32), halo_v[0, rows, :].astype(F32))
        high = jnp.where(spot < 96, halo_v[3, rows, :].astype(F32), halo_v[2, rows, :].astype(F32))
        halo = jnp.where(spot < 64, low, high).astype(BF)
        added = jnp.dot(halo, halo_map_v[...], preferred_element_type=F32)
        blended = base_v[c * CH : (c + 1) * CH, :] + on_rows(damping_v[0]) * added
        h_v[rows, :] = jnp.where(active_of(r, c), blended, 0.0).astype(BF)

        if relaying:

            @pl.when((r < ROUNDS - 1) & has_down & (depth != CROSS_FROM))
            def _():
                down_copy(t).start()

            @pl.when((r < ROUNDS - 1) & (depth == CROSS_FROM))
            def _():
                for q in range(len(CROSS_VIA)):
                    to_relay(t, q).start()
                if first and c < CHUNKS - 1 or 0 < c < CHUNKS - 1:
                    down_copy(t, 0).start()

        else:

            @pl.when((r < ROUNDS - 1) & has_down)
            def _():
                down_copy(t).start()

        @pl.when(r == ROUNDS - 1)
        def _():
            out_copy(t, c).start()

    def out_copy(t, c):
        return pltpu.make_async_copy(
            h_v.at[rows_of(t)], out_ref.at[pl.ds(c * CH, CH)], out_sem.at[c]
        )

    for one in loads[:3]:
        one.wait()

    def one_round(r, first):
        lag = 2 if first else 1
        for c in range(CHUNKS):
            advance(r, c, first)
            if c < CHUNKS - 1 and not first:
                pass_on(r - 1, c + 1)
            if c == lag and first:
                rows = jnp.dot(halo_sel_v[...], second_v[...], preferred_element_type=F32)
                halo_map_v[...] = (coupling_weight * rows).astype(BF)
            if c >= lag:
                finish(r, c - lag, first)
        for c in range(CHUNKS - lag, CHUNKS):
            if c == CHUNKS - 1:
                pass_on(r, 0)
            finish(r, c, first)

    one_round(jnp.int32(0), True)
    for r in range(1, ROUNDS):
        fill_pick(r)
    columns = jnp.dot(first_v[...], face_sel_v[...], preferred_element_type=F32)
    first_faces_v[...] = columns.astype(BF)
    loads[4].wait()

    def drain_faces(t, carry):
        for k, (_, _, there) in enumerate(sides):

            @pl.when(there)
            def _():
                face_copy(k, t).wait_send()

        return carry

    def later_round(r, carry):
        lax.fori_loop((r - 1) * CHUNKS, r * CHUNKS, drain_faces, 0)
        one_round(r, False)
        return carry

    lax.fori_loop(1, ROUNDS, later_round, 0)
    lax.fori_loop((ROUNDS - 1) * CHUNKS, ROUNDS * CHUNKS, drain_faces, 0)

    def drain_down(r, carry):
        for c in range(CHUNKS):
            t = r * CHUNKS + c
            if relaying:

                @pl.when(has_down & (depth != CROSS_FROM))
                def _():
                    down_copy(t).wait_send()

                @pl.when(depth == CROSS_FROM)
                def _():
                    down_copy(t, 0).wait_send()
                    for q in range(len(CROSS_VIA)):
                        to_relay(t, q).wait_send()

                for q, via in enumerate(CROSS_VIA):

                    @pl.when(depth == via)
                    def _():
                        from_relay(t, q).wait_send()

            else:

                @pl.when(has_down)
                def _():
                    down_copy(t).wait_send()

        return carry

    lax.fori_loop(0, ROUNDS - 1, drain_down, 0)

    for c in range(CHUNKS):
        out_copy((ROUNDS - 1) * CHUNKS + c, c).wait()


def local(arrival, source, assignment, counts, first_map, second_map, damping):
    steps = ROUNDS * CHUNKS
    slots = ROUNDS * SLOTS
    anywhere = pl.BlockSpec(memory_space=pl.ANY)
    vmem = pl.BlockSpec(memory_space=pltpu.VMEM)
    dma = pltpu.SemaphoreType.DMA
    units, batches = counts.shape[:2]
    result = pl.pallas_call(
        kernel,
        out_shape=pltpu.VMEM((SLOTS, M), BF),
        in_specs=[
            anywhere,
            anywhere,
            vmem,
            pl.BlockSpec(memory_space=pltpu.SMEM),
            anywhere,
            anywhere,
            vmem,
        ],
        out_specs=anywhere,
        scratch_shapes=[
            pltpu.VMEM((slots, M), BF),
            pltpu.VMEM((slots, M), BF),
            pltpu.VMEM((M, M), BF),
            pltpu.VMEM((M, M), BF),
            pltpu.VMEM((slots, SLOTS), BF),
            pltpu.VMEM((M, LANES), BF),
            pltpu.VMEM((LANES, M), BF),
            pltpu.VMEM((M, LANES), BF),
            pltpu.VMEM((LANES, M), BF),
            pltpu.VMEM((4, 8, M), F32),
            pltpu.VMEM((2, 8, M), F32),
            pltpu.VMEM((SLOTS, M), F32),
            pltpu.VMEM((slots, LANES), BF),
            pltpu.VMEM((4, slots, LANES), BF),
            pltpu.VMEM((slots, M), BF),
            pltpu.VMEM((steps * SHARE, M), BF),
            dma((5,)),
            dma((4, steps)),
            dma((4, steps)),
            dma((steps,)),
            dma((steps,)),
            dma((len(CROSS_VIA), steps)),
            dma((steps,)),
            dma((steps,)),
            dma((len(CROSS_VIA), steps)),
            dma((CHUNKS,)),
        ],
        compiler_params=pltpu.CompilerParams(
            collective_id=0, has_side_effects=True, vmem_limit_bytes=60_000_000
        ),
        name="sweep",
    )(
        arrival.reshape(SLOTS, M),
        source.reshape(slots, M),
        assignment,
        counts.reshape(units, 1, batches),
        first_map.reshape(M, M),
        second_map.reshape(M, M),
        damping.reshape(1, M),
    )
    return result.reshape(1, SLOTS, 1, 1, M)


def solution(mesh):
    return jax.shard_map(
        local,
        mesh=mesh,
        in_specs=(
            P("depth", None, "gx", "gy", None),
            P("depth", None, None, "gx", "gy", None),
            P(),
            P(None, None, "gx", "gy"),
            P("depth", "gx", "gy", None, None),
            P("depth", "gx", "gy", None, None),
            P("depth", "gx", "gy", None),
        ),
        out_specs=P("depth", None, "gx", "gy", None),
        check_vma=False,
    )
```
